32 devices in a mesh: brow: 4 (over y, x), bcol: 8 (over z, core).
Axes of the slice: x: 2, y: 2, z: 4, core: 2. Of those that a mesh axis runs over, the one named last changes fastest.
Arguments:
- gradient: bfloat16 [2048, 2048], P(('brow', 'bcol')), may hold values from -1.5 to 1.5
- left_stats: float32 [4, 2048, 512], P('brow', 'bcol'), may hold values from -1 to 8, as said below
- right_stats: float32 [4, 2048, 512], P('brow', 'bcol'), may hold values from -1 to 8, as said below
- left_roots: bfloat16 [4, 2048, 512], P('brow', 'bcol'), may hold values from -1 to 3, as said below
- right_roots: bfloat16 [4, 2048, 512], P('brow', 'bcol'), may hold values from -1 to 3, as said below
- refresh: int32 [4, 1], P('brow'), may hold values from 0 to 3, as said below
Outputs:
- update: bfloat16 [2048, 2048], P(('brow', 'bcol'))
- new_left_stats: float32 [4, 2048, 512], P('brow', 'bcol')
- new_right_stats: float32 [4, 2048, 512], P('brow', 'bcol')
- new_left_roots: bfloat16 [4, 2048, 512], P('brow', 'bcol')
- new_right_roots: bfloat16 [4, 2048, 512], P('brow', 'bcol')
The draws below stay inside these ranges and needn't reach their ends.
Inputs may be any that keep to these rules, and one draw needn't show every extreme that they name: `refresh`: each row names 1 different block columns; some block row lists column 3 and another block row lists column 0. `left_stats`: every 512 x 512 block is symmetric positive definite. `right_stats`: every 512 x 512 block is symmetric positive definite. `left_roots`: every 512 x 512 block is symmetric. `right_roots`: every 512 x 512 block is symmetric.
All inputs are finite; a program needn't handle non-finite values.
Results may differ from the reference program's by a relative error of at most 0.005.
Values may be sent and summed in bfloat16 or wider, within the bound.
No kernel may reach another device: no remote copies, remote signals or barrier semaphores. Data moves between devices by JAX's collectives and lax.ppermute only.
A program may use at most 64 MiB of HBM per device.

```python
import math
import jax
import jax.numpy as jnp
from jax import lax

B = 512
ITERS = 3
ROW_BLOCKS = 4
COL_BLOCKS = 4
LISTED = 1
ROWS = 2048
COLS = 2048


def symmetric_blocks(key, lowest, highest_value, spread):
    first_key, second_key = jax.random.split(key)
    noise = jax.random.normal(first_key, (ROW_BLOCKS, COL_BLOCKS, B, B), jnp.float32)
    noise = (noise + jnp.swapaxes(noise, 2, 3)) * (spread / math.sqrt(2.0 * B))
    diagonal = jnp.exp(jax.random.uniform(second_key, (ROW_BLOCKS, COL_BLOCKS, B), jnp.float32, math.log(lowest), math.log(highest_value)))
    identity = jnp.eye(B, dtype=jnp.float32)
    matrix = noise + diagonal[..., None] * identity
    return matrix.reshape(ROW_BLOCKS, COL_BLOCKS * B, B)


def draw_left_stats(key, part):
    return symmetric_blocks(jax.random.fold_in(key, 11), 1.0, 3.0, 0.4)


def draw_right_stats(key, part):
    return symmetric_blocks(jax.random.fold_in(key, 23), 1.0, 3.0, 0.4)


def draw_left_roots(key, part):
    return symmetric_blocks(jax.random.fold_in(key, 37), 0.5, 1.5, 0.25).astype(jnp.bfloat16)


def draw_right_roots(key, part):
    return symmetric_blocks(jax.random.fold_in(key, 41), 0.5, 1.5, 0.25).astype(jnp.bfloat16)


def bring_front(order, target):
    moved = jnp.where(order == target, order[0], order)
    return moved.at[0].set(target)


def draw_refresh(key, part):
    row_keys = jax.random.split(jax.random.fold_in(key, 53), ROW_BLOCKS)
    orders = jax.vmap(lambda row_key: jax.random.permutation(row_key, COL_BLOCKS))(row_keys)
    orders = orders.astype(jnp.int32)
    first_key, second_key = jax.random.split(jax.random.fold_in(key, 61))
    first_row = jax.random.randint(first_key, (), 0, ROW_BLOCKS, dtype=jnp.int32)
    offset = jax.random.randint(second_key, (), 1, ROW_BLOCKS, dtype=jnp.int32)
    second_row = (first_row + offset) % ROW_BLOCKS
    last_target = jnp.full((ROW_BLOCKS,), COL_BLOCKS - 1, dtype=jnp.int32)
    zero_target = jnp.zeros((ROW_BLOCKS,), dtype=jnp.int32)
    front_last = jax.vmap(bring_front)(orders, last_target)
    front_zero = jax.vmap(bring_front)(orders, zero_target)
    row_ids = jnp.arange(ROW_BLOCKS, dtype=jnp.int32)[:, None]
    orders = jnp.where(row_ids == first_row, front_last, orders)
    orders = jnp.where(row_ids == second_row, front_zero, orders)
    return orders[:, :LISTED].astype(jnp.int32)


def block_scale(own_key, dims, shards, smallest, high):
    gain, own = 1.0, jax.random.fold_in(own_key, 6)
    for position, parts in shards:
        heights = jnp.exp(jax.random.uniform(jax.random.fold_in(own, position), (parts,), jnp.float32, smallest / len(shards), high / len(shards)))
        gain = gain * jnp.repeat(heights, dims[position] // parts).reshape([-1 if axis == position else 1 for axis in range(len(dims))])
    return gain


def scatter_about(own_key, dims, deviation, most, cuts=(), held_as=jnp.bfloat16):
    factor_of = block_scale(own_key, dims, cuts, -0.22, 0.18) if cuts else 1.0
    values = jax.random.normal(own_key, dims, jnp.float32) * deviation * factor_of
    return jnp.minimum(jnp.maximum(values, -most), most).astype(held_as)


def setup_inputs(seed: int = 0) -> dict:
    keys = jax.random.split(jax.random.key(seed), 7)
    return {
        "gradient": scatter_about(keys[0], (ROWS, COLS), 0.25, 1.5, ((0, 32),)),
        "left_stats": draw_left_stats(jax.random.fold_in(keys[6], 71), 0),
        "right_stats": draw_right_stats(jax.random.fold_in(keys[6], 71), 0),
        "left_roots": draw_left_roots(jax.random.fold_in(keys[6], 71), 0),
        "right_roots": draw_right_roots(jax.random.fold_in(keys[6], 71), 0),
        "refresh": draw_refresh(jax.random.fold_in(keys[6], 71), 0),
    }


decay = 0.9
epsilon = 1e-06
highest = lax.Precision.HIGHEST

def inverse_root(matrix):
    order_size = matrix.shape[0]
    identity = jnp.eye(order_size, dtype=jnp.float32)
    shifted = matrix + epsilon * identity
    scaling = 2.5 / jnp.sqrt(jnp.sum(shifted * shifted))
    moment = scaling * shifted
    iterate = jnp.sqrt(jnp.sqrt(scaling)) * identity
    for iteration in range(ITERS):
        factor = (5.0 * identity - moment) * 0.25
        square = jnp.dot(factor, factor, precision=highest)
        fourth = jnp.dot(square, square, precision=highest)
        moment = jnp.dot(fourth, moment, precision=highest)
        iterate = jnp.dot(iterate, factor, precision=highest)
    return iterate.astype(jnp.bfloat16)

def refresh_row(row_items):
    left_row, right_row, chosen, left_old_root, right_old_root = row_items
    picked = jnp.concatenate([left_row[chosen], right_row[chosen]], 0)
    new_roots = lax.map(inverse_root, picked).astype(jnp.float32)
    one_hot = (chosen[:, None] == jnp.arange(COL_BLOCKS, dtype=jnp.int32)[None, :]).astype(jnp.float32)
    listed = lax.optimization_barrier(jnp.sum(one_hot, 0)) > 0
    left_fresh = jnp.einsum('sc,sij->cij', one_hot, new_roots[:LISTED], precision=highest)
    right_fresh = jnp.einsum('sc,sij->cij', one_hot, new_roots[LISTED:], precision=highest)
    left_out = jnp.where(listed[:, None, None], left_fresh, left_old_root.astype(jnp.float32))
    right_out = jnp.where(listed[:, None, None], right_fresh, right_old_root.astype(jnp.float32))
    return (left_out.astype(jnp.bfloat16), right_out.astype(jnp.bfloat16))

def reference(gradient, left_stats, right_stats, left_roots, right_roots, refresh):
    blocks = gradient.reshape(ROW_BLOCKS, B, COL_BLOCKS, B).transpose(0, 2, 1, 3).astype(jnp.float32)
    left_old = left_stats.reshape(ROW_BLOCKS, COL_BLOCKS, B, B)
    right_old = right_stats.reshape(ROW_BLOCKS, COL_BLOCKS, B, B)
    left_gram = jnp.einsum('rcik,rcjk->rcij', blocks, blocks, precision=highest)
    right_gram = jnp.einsum('rcki,rckj->rcij', blocks, blocks, precision=highest)
    left_new = decay * left_old + (1.0 - decay) * left_gram
    right_new = decay * right_old + (1.0 - decay) * right_gram
    left_root_blocks = left_roots.reshape(ROW_BLOCKS, COL_BLOCKS, B, B)
    right_root_blocks = right_roots.reshape(ROW_BLOCKS, COL_BLOCKS, B, B)
    mixed = jnp.einsum('rcik,rckj->rcij', blocks, right_root_blocks.astype(jnp.float32), precision=highest)
    mixed = lax.optimization_barrier(mixed.astype(jnp.bfloat16)).astype(jnp.float32)
    update = jnp.einsum('rcik,rckj->rcij', left_root_blocks.astype(jnp.float32), mixed, precision=highest)
    update = update.astype(jnp.bfloat16).transpose(0, 2, 1, 3).reshape(ROWS, COLS)
    left_out, right_out = lax.map(refresh_row, (left_new, right_new, refresh, left_root_blocks, right_root_blocks))
    shape_out = (ROW_BLOCKS, COL_BLOCKS * B, B)
    return (update, left_new.reshape(shape_out), right_new.reshape(shape_out), left_out.reshape(shape_out), right_out.reshape(shape_out))
```

```python
import jax
import jax.numpy as jnp
from jax import lax
from jax.experimental import pallas as pl
from jax.experimental.pallas import tpu as pltpu
from jax.sharding import PartitionSpec as P

ITERS = 3
decay = 0.9
epsilon = 1e-06
F32 = jnp.float32
BF16 = jnp.bfloat16
VMEM = pl.BlockSpec(memory_space=pltpu.VMEM)
SMEM = pl.BlockSpec(memory_space=pltpu.SMEM)


def place():
    position = lax.axis_index("bcol")
    return position >> 1, position & 1


def chip_pairs(step):
    return [(i, i ^ (step << 1)) for i in range(lax.axis_size("bcol"))]


def core_pairs():
    return [(i, i ^ 1) for i in range(lax.axis_size("bcol"))]


def dot(left_side, right_side, contract=((1,), (0,))):
    return lax.dot_general(left_side, right_side, (contract, ((), ())), preferred_element_type=F32)


def call(kernel, out_shape, scratch, cost, name):
    flops, moved = cost
    return lambda *operands: pl.pallas_call(
        kernel,
        out_shape=out_shape,
        in_specs=[SMEM if o.dtype == jnp.int32 else VMEM for o in operands],
        out_specs=jax.tree.map(lambda _: VMEM, out_shape),
        scratch_shapes=scratch,
        name=name,
        cost_estimate=pl.CostEstimate(flops=flops, bytes_accessed=moved, transcendentals=0),
    )(*operands)


def prepare(chips, rows, order, left_mine, left_other, right_mine, right_other, old_left, old_right, old_other,
            left_rows, right_full, side, left_full):
    column, half = place()
    span = order // 2
    mine = pl.ds(pl.multiple_of(half * span, span), span)
    other = pl.ds(pl.multiple_of((1 - half) * span, span), span)
    left_full[mine, :] = left_mine[...]
    left_full[other, :] = left_other[...]
    right_full[mine, :] = right_mine[...]
    right_full[other, :] = right_other[...]
    for step in range(chips):
        start = pl.multiple_of(((column ^ step) * 2 + half) * rows, rows)
        left_rows[step * rows : (step + 1) * rows, :] = left_full[pl.ds(start, rows), :]
    side[other, :] = old_other[...]


def precondition(chips, rows, order, *refs):
    mine, other = refs[:chips], refs[chips : 2 * chips]
    left_rows, right_full = refs[2 * chips : 2 * chips + 2]
    updates, whole = refs[2 * chips + 2 : 3 * chips + 2], refs[3 * chips + 2]
    column, half = place()
    for step in range(chips):
        start = (column ^ step) * 2
        whole[pl.ds(pl.multiple_of((start + half) * rows, rows), rows), :] = mine[step][...]
        whole[pl.ds(pl.multiple_of((start + 1 - half) * rows, rows), rows), :] = other[step][...]
    mixed = dot(whole[...], right_full[...]).astype(BF16)
    result = dot(left_rows[...], mixed).astype(BF16)
    for step in range(chips):
        updates[step][...] = result[step * rows : (step + 1) * rows, :]


def refreshed(order, whole, old_left, old_right, old_side, new_left, new_right, root_mine, root_other, stat, weight, root):
    column, half = place()
    span = order // 2
    mine = pl.ds(pl.multiple_of(half * span, span), span)
    other = pl.ds(pl.multiple_of((1 - half) * span, span), span)
    rate = 1.0 - decay
    full = whole[...]
    new_left[...] = decay * old_left[...] + rate * dot(whole[mine, :], full, ((1,), (1,)))
    new_right[...] = decay * old_right[...] + rate * dot(whole[:, mine], full, ((0,), (0,)))

    @pl.when(half == 0)
    def _():
        stat[mine, :] = new_left[...]
        stat[other, :] = decay * old_side[other, :] + rate * dot(whole[other, :], full, ((1,), (1,)))

    @pl.when(half == 1)
    def _():
        stat[mine, :] = new_right[...]
        stat[other, :] = decay * old_side[other, :] + rate * dot(whole[:, other], full, ((0,), (0,)))

    shape = (order, order)
    diagonal = lax.broadcasted_iota(jnp.int32, shape, 0) == lax.broadcasted_iota(jnp.int32, shape, 1)
    shifted = stat[...] + jnp.where(diagonal, epsilon, 0.0)
    total = jnp.sum(jnp.sum(shifted * shifted, axis=1, keepdims=True), axis=0, keepdims=True)
    scaling = 2.5 / jnp.sqrt(total)
    stat[...] = scaling * shifted
    held = 1.25
    weight[...] = -0.25 * stat[...]
    square = 25.0 / 16.0
    for iteration in range(1, ITERS):
        moment = stat[...]
        narrow = moment.astype(BF16)
        change = (dot(narrow, narrow) - 10.0 * moment) * (1.0 / 16.0)
        small = change.astype(BF16)
        fourth = (2.0 * square) * change + dot(small, small)
        moment = (square * square) * moment + dot(fourth.astype(BF16), narrow)
        stat[...] = moment
        product = dot(weight[...].astype(BF16), moment.astype(BF16))
        weight[...] = 1.25 * weight[...] - (0.25 * held) * moment - 0.25 * product
        held = 1.25 * held
    scale = jnp.sqrt(jnp.sqrt(scaling))
    root[...] = (scale * (weight[...] + jnp.where(diagonal, held, 0.0))).astype(BF16)
    root_mine[...] = root[mine, :]
    root_other[...] = root[other, :]


def body(gradient, left_stats, right_stats, left_roots, right_roots, refresh):
    column, half = place()
    chips = lax.axis_size("bcol") // 2
    rows = gradient.shape[0]
    order = left_stats.shape[2]
    span = order // 2
    is_second = half == 1
    left_old, right_old = left_stats[0], right_stats[0]
    left_root, right_root = left_roots[0], right_roots[0]

    def piece(step):
        return lax.dynamic_slice(gradient, (0, (column ^ step) * order), (rows, order))

    pieces = [piece(step) for step in range(chips)]
    mine = [pieces[0]] + [lax.ppermute(pieces[step], "bcol", chip_pairs(step)) for step in range(1, chips)]
    given_stat = jnp.where(is_second, left_old, right_old).astype(BF16)
    left_other, right_other, old_other = [
        lax.ppermute(x, "bcol", core_pairs()) for x in (left_root, right_root, given_stat)
    ]
    other = [lax.ppermute(x, "bcol", core_pairs()) for x in mine]

    def shape(r, c, t):
        return jax.ShapeDtypeStruct((r, c), t)

    def kernel(f, *static):
        return lambda *refs: f(*static, *refs)

    left_rows, right_full, old_side = call(
        kernel(prepare, chips, rows, order),
        (shape(span, order, BF16), shape(order, order, BF16), shape(order, order, F32)),
        [pltpu.VMEM((order, order), BF16)],
        (0, 4 * order * order * 2),
        "prepare",
    )(left_root, left_other, right_root, right_other, left_old, right_old, old_other.astype(F32))
    *updates, whole = call(
        kernel(precondition, chips, rows, order),
        (*[shape(rows, order, BF16)] * chips, shape(order, order, BF16)),
        [],
        (3 * order**3, 4 * order * order * 2),
        "precondition",
    )(*mine, *other, left_rows, right_full)
    returned = [updates[0]] + [lax.ppermute(updates[step], "bcol", chip_pairs(step)) for step in range(1, chips)]
    left_new, right_new, root_mine, root_other = call(
        kernel(refreshed, order),
        (shape(span, order, F32), shape(span, order, F32), shape(span, order, BF16), shape(span, order, BF16)),
        [pltpu.VMEM((order, order), F32), pltpu.VMEM((order, order), F32), pltpu.VMEM((order, order), BF16)],
        (20 * order**3, 8 * order * order * 4),
        "refreshed",
    )(whole, left_old, right_old, old_side)
    taken = lax.ppermute(root_other, "bcol", core_pairs())
    listed = jnp.any(refresh[0] == column)
    left_out = jnp.where(listed, jnp.where(is_second, taken, root_mine), left_root)
    right_out = jnp.where(listed, jnp.where(is_second, root_mine, taken), right_root)
    update = jnp.zeros((rows, chips * order), BF16)
    for step in range(chips):
        update = lax.dynamic_update_slice(update, returned[step], (0, (column ^ step) * order))
    return (update, left_new[None], right_new[None], left_out[None], right_out[None])


def solution(mesh):
    block = P("brow", "bcol", None)
    rows = P(("brow", "bcol"), None)
    in_specs = (rows, block, block, block, block, P("brow", None))
    out_specs = (rows, block, block, block, block)
    return jax.shard_map(body, mesh=mesh, in_specs=in_specs, out_specs=out_specs, check_vma=False)
```

```python
import jax
import jax.numpy as jnp
from jax import lax
from jax.experimental import pallas as pl
from jax.experimental.pallas import tpu as pltpu
from jax.sharding import PartitionSpec as P

ITERS = 3
decay = 0.9
epsilon = 1e-06
F32 = jnp.float32
BF16 = jnp.bfloat16
VMEM = pl.BlockSpec(memory_space=pltpu.VMEM)
SMEM = pl.BlockSpec(memory_space=pltpu.SMEM)


def place():
    position = lax.axis_index("bcol")
    return position >> 1, position & 1


def chip_pairs(step):
    return [(i, i ^ (step << 1)) for i in range(lax.axis_size("bcol"))]


def core_pairs():
    return [(i, i ^ 1) for i in range(lax.axis_size("bcol"))]


def dot(left_side, right_side, contract=((1,), (0,))):
    return lax.dot_general(left_side, right_side, (contract, ((), ())), preferred_element_type=F32)


def call(kernel, out_shape, scratch, cost, name):
    flops, moved = cost
    return lambda *operands: pl.pallas_call(
        kernel,
        out_shape=out_shape,
        in_specs=[SMEM if o.dtype == jnp.int32 else VMEM for o in operands],
        out_specs=jax.tree.map(lambda _: VMEM, out_shape),
        scratch_shapes=scratch,
        name=name,
        compiler_params=pltpu.CompilerParams(vmem_limit_bytes=16 << 20),
        cost_estimate=pl.CostEstimate(flops=flops, bytes_accessed=moved, transcendentals=0),
    )(*operands)


def prepare(chips, rows, order, left_mine, left_other, right_mine, right_other, old_left, old_right, old_other,
            left_rows, right_full, side, left_full):
    column, half = place()
    span = order // 2
    mine = pl.ds(pl.multiple_of(half * span, span), span)
    other = pl.ds(pl.multiple_of((1 - half) * span, span), span)
    left_full[mine, :] = left_mine[...]
    left_full[other, :] = left_other[...]
    right_full[mine, :] = right_mine[...]
    right_full[other, :] = right_other[...]
    for step in range(chips):
        start = pl.multiple_of(((column ^ step) * 2 + half) * rows, rows)
        left_rows[step * rows : (step + 1) * rows, :] = left_full[pl.ds(start, rows), :]
    side[other, :] = old_other[...]


def precondition(chips, rows, order, *refs):
    mine, other = refs[:chips], refs[chips : 2 * chips]
    left_rows, right_full = refs[2 * chips : 2 * chips + 2]
    updates, whole = refs[2 * chips + 2 : 3 * chips + 2], refs[3 * chips + 2]
    column, half = place()
    for step in range(chips):
        start = (column ^ step) * 2
        whole[pl.ds(pl.multiple_of((start + half) * rows, rows), rows), :] = mine[step][...]
        whole[pl.ds(pl.multiple_of((start + 1 - half) * rows, rows), rows), :] = other[step][...]
    mixed = dot(whole[...], right_full[...]).astype(BF16)
    result = dot(left_rows[...], mixed).astype(BF16)
    for step in range(chips):
        updates[step][...] = result[step * rows : (step + 1) * rows, :]


def refreshed(order, whole, old_left, old_right, old_side, new_left, new_right, root_mine, root_other, stat, weight, root):
    column, half = place()
    span = order // 2
    mine = pl.ds(pl.multiple_of(half * span, span), span)
    other = pl.ds(pl.multiple_of((1 - half) * span, span), span)
    rate = 1.0 - decay
    full = whole[...]
    new_left[...] = decay * old_left[...] + rate * dot(whole[mine, :], full, ((1,), (1,)))
    new_right[...] = decay * old_right[...] + rate * dot(whole[:, mine], full, ((0,), (0,)))

    @pl.when(half == 0)
    def _():
        stat[mine, :] = new_left[...]
        stat[other, :] = decay * old_side[other, :] + rate * dot(whole[other, :], full, ((1,), (1,)))

    @pl.when(half == 1)
    def _():
        stat[mine, :] = new_right[...]
        stat[other, :] = decay * old_side[other, :] + rate * dot(whole[:, other], full, ((0,), (0,)))

    shape = (order, order)
    diagonal = lax.broadcasted_iota(jnp.int32, shape, 0) == lax.broadcasted_iota(jnp.int32, shape, 1)
    shifted = stat[...] + jnp.where(diagonal, epsilon, 0.0)
    total = jnp.sum(jnp.sum(shifted * shifted, axis=1, keepdims=True), axis=0, keepdims=True)
    scaling = 2.5 / jnp.sqrt(total)
    stat[...] = scaling * shifted
    held = 1.25
    weight[...] = -0.25 * stat[...]
    square = 25.0 / 16.0
    for iteration in range(1, ITERS):
        moment = stat[...]
        narrow = moment.astype(BF16)
        change = (dot(narrow, narrow) - 10.0 * moment) * (1.0 / 16.0)
        small = change.astype(BF16)
        fourth = (2.0 * square) * change + dot(small, small)
        moment = (square * square) * moment + dot(fourth.astype(BF16), narrow)
        stat[...] = moment
        product = dot(weight[...].astype(BF16), moment.astype(BF16))
        weight[...] = 1.25 * weight[...] - (0.25 * held) * moment - 0.25 * product
        held = 1.25 * held
    scale = jnp.sqrt(jnp.sqrt(scaling))
    root[...] = (scale * (weight[...] + jnp.where(diagonal, held, 0.0))).astype(BF16)
    root_mine[...] = root[mine, :]
    root_other[...] = root[other, :]


def body(gradient, left_stats, right_stats, left_roots, right_roots, refresh):
    column, half = place()
    chips = lax.axis_size("bcol") // 2
    rows = gradient.shape[0]
    order = left_stats.shape[2]
    span = order // 2
    is_second = half == 1
    left_old, right_old = left_stats[0], right_stats[0]
    left_root, right_root = left_roots[0], right_roots[0]

    def piece(step):
        return lax.dynamic_slice(gradient, (0, (column ^ step) * order), (rows, order))

    pieces = [piece(step) for step in range(chips)]
    mine = [pieces[0]] + [lax.ppermute(pieces[step], "bcol", chip_pairs(step)) for step in range(1, chips)]
    given_stat = jnp.where(is_second, left_old, right_old).astype(BF16)
    left_other, right_other, old_other = [
        lax.ppermute(x, "bcol", core_pairs()) for x in (left_root, right_root, given_stat)
    ]
    other = [lax.ppermute(x, "bcol", core_pairs()) for x in mine]

    def shape(r, c, t):
        return jax.ShapeDtypeStruct((r, c), t)

    def kernel(f, *static):
        return lambda *refs: f(*static, *refs)

    left_rows, right_full, old_side = call(
        kernel(prepare, chips, rows, order),
        (shape(span, order, BF16), shape(order, order, BF16), shape(order, order, F32)),
        [pltpu.VMEM((order, order), BF16)],
        (0, 4 * order * order * 2),
        "prepare",
    )(left_root, left_other, right_root, right_other, left_old, right_old, old_other.astype(F32))
    *updates, whole = call(
        kernel(precondition, chips, rows, order),
        (*[shape(rows, order, BF16)] * chips, shape(order, order, BF16)),
        [],
        (3 * order**3, 4 * order * order * 2),
        "precondition",
    )(*mine, *other, left_rows, right_full)
    returned = [updates[0]] + [lax.ppermute(updates[step], "bcol", chip_pairs(step)) for step in range(1, chips)]
    left_new, right_new, root_mine, root_other = call(
        kernel(refreshed, order),
        (shape(span, order, F32), shape(span, order, F32), shape(span, order, BF16), shape(span, order, BF16)),
        [pltpu.VMEM((order, order), F32), pltpu.VMEM((order, order), F32), pltpu.VMEM((order, order), BF16)],
        (20 * order**3, 8 * order * order * 4),
        "refreshed",
    )(whole, left_old, right_old, old_side)
    taken = lax.ppermute(root_other, "bcol", core_pairs())
    listed = jnp.any(refresh[0] == column)
    left_out = jnp.where(listed, jnp.where(is_second, taken, root_mine), left_root)
    right_out = jnp.where(listed, jnp.where(is_second, root_mine, taken), right_root)
    update = jnp.zeros((rows, chips * order), BF16)
    for step in range(chips):
        update = lax.dynamic_update_slice(update, returned[step], (0, (column ^ step) * order))
    return (update, left_new[None], right_new[None], left_out[None], right_out[None])


def solution(mesh):
    block = P("brow", "bcol", None)
    rows = P(("brow", "bcol"), None)
    in_specs = (rows, block, block, block, block, P("brow", None))
    out_specs = (rows, block, block, block, block)
    return jax.shard_map(body, mesh=mesh, in_specs=in_specs, out_specs=out_specs, check_vma=False)
```

```python
import jax
import jax.numpy as jnp
from jax import lax
from jax.experimental import pallas as pl
from jax.experimental.pallas import tpu as pltpu
from jax.sharding import PartitionSpec as P

ITERS = 3
decay = 0.9
epsilon = 1e-06
F32 = jnp.float32
BF16 = jnp.bfloat16
VMEM = pl.BlockSpec(memory_space=pltpu.VMEM)
SMEM = pl.BlockSpec(memory_space=pltpu.SMEM)


def place():
    position = lax.axis_index("bcol")
    return position >> 1, position & 1


def chip_pairs(step):
    return [(i, i ^ (step << 1)) for i in range(lax.axis_size("bcol"))]


def core_pairs():
    return [(i, i ^ 1) for i in range(lax.axis_size("bcol"))]


def permute(value, pairs):
    return lax.ppermute(value, "bcol", pairs)


def dot(left_side, right_side, contract=((1,), (0,))):
    return lax.dot_general(left_side, right_side, (contract, ((), ())), preferred_element_type=F32)


def call(kernel, out_shape, scratch, cost):
    flops, moved = cost

    def run(*operands):
      return pl.pallas_call(
        kernel,
        out_shape=out_shape,
        in_specs=[SMEM if o.dtype == jnp.int32 else VMEM for o in operands],
        out_specs=jax.tree.map(lambda _: VMEM, out_shape),
        scratch_shapes=scratch,
        compiler_params=pltpu.CompilerParams(vmem_limit_bytes=16 << 20),
        cost_estimate=pl.CostEstimate(flops=flops, bytes_accessed=moved, transcendentals=0),
    )(*operands)

    return run


def prepare(chips, rows, order, left_mine, left_other, right_mine, right_other, old_left, old_right, old_other,
            left_rows, right_full, side, left_full):
    column, half = place()
    span = order // 2
    mine = pl.ds(pl.multiple_of(half * span, span), span)
    other = pl.ds(pl.multiple_of((1 - half) * span, span), span)
    left_full[mine, :] = left_mine[...]
    left_full[other, :] = left_other[...]
    right_full[mine, :] = right_mine[...]
    right_full[other, :] = right_other[...]
    for step in range(chips):
        start = pl.multiple_of(((column ^ step) * 2 + half) * rows, rows)
        left_rows[step * rows : (step + 1) * rows, :] = left_full[pl.ds(start, rows), :]
    side[other, :] = old_other[...]


def precondition(chips, rows, order, *refs):
    mine, other = refs[:chips], refs[chips : 2 * chips]
    left_rows, right_full = refs[2 * chips : 2 * chips + 2]
    updates, whole = refs[2 * chips + 2 : 3 * chips + 2], refs[3 * chips + 2]
    column, half = place()
    for step in range(chips):
        start = (column ^ step) * 2
        whole[pl.ds(pl.multiple_of((start + half) * rows, rows), rows), :] = mine[step][...]
        whole[pl.ds(pl.multiple_of((start + 1 - half) * rows, rows), rows), :] = other[step][...]
    mixed = dot(whole[...], right_full[...]).astype(BF16)
    result = dot(left_rows[...], mixed).astype(BF16)
    for step in range(chips):
        updates[step][...] = result[step * rows : (step + 1) * rows, :]


def refreshed(order, whole, old_left, old_right, old_side, new_left, new_right, root_mine, root_other, stat, weight, root):
    _, half = place()
    span = order // 2
    mine = pl.ds(pl.multiple_of(half * span, span), span)
    other = pl.ds(pl.multiple_of((1 - half) * span, span), span)
    rate = 1.0 - decay
    full = whole[...]
    new_left[...] = decay * old_left[...] + rate * dot(whole[mine, :], full, ((1,), (1,)))
    new_right[...] = decay * old_right[...] + rate * dot(whole[:, mine], full, ((0,), (0,)))

    @pl.when(half == 0)
    def _():
        stat[mine, :] = new_left[...]
        stat[other, :] = decay * old_side[other, :] + rate * dot(whole[other, :], full, ((1,), (1,)))

    @pl.when(half == 1)
    def _():
        stat[mine, :] = new_right[...]
        stat[other, :] = decay * old_side[other, :] + rate * dot(whole[:, other], full, ((0,), (0,)))

    shape = (order, order)
    diagonal = lax.broadcasted_iota(jnp.int32, shape, 0) == lax.broadcasted_iota(jnp.int32, shape, 1)
    shifted = stat[...] + jnp.where(diagonal, epsilon, 0.0)
    total = jnp.sum(jnp.sum(shifted * shifted, axis=1, keepdims=True), axis=0, keepdims=True)
    scaling = 2.5 / jnp.sqrt(total)
    stat[...] = scaling * shifted
    held = 1.25
    weight[...] = -0.25 * stat[...]
    square = 25.0 / 16.0
    for _ in range(1, ITERS):
        moment = stat[...]
        narrow = moment.astype(BF16)
        change = (dot(narrow, narrow) - 10.0 * moment) * (1.0 / 16.0)
        small = change.astype(BF16)
        fourth = (2.0 * square) * change + dot(small, small)
        moment = (square * square) * moment + dot(fourth.astype(BF16), narrow)
        stat[...] = moment
        product = dot(weight[...].astype(BF16), moment.astype(BF16))
        weight[...] = 1.25 * weight[...] - (0.25 * held) * moment - 0.25 * product
        held = 1.25 * held
    scale = jnp.sqrt(jnp.sqrt(scaling))
    root[...] = (scale * (weight[...] + jnp.where(diagonal, held, 0.0))).astype(BF16)
    root_mine[...] = root[mine, :]
    root_other[...] = root[other, :]


def step(gradient, left_stats, right_stats, left_roots, right_roots, refresh):
    column, half = place()
    chips = lax.axis_size("bcol") // 2
    rows = gradient.shape[0]
    order = left_stats.shape[2]
    span = order // 2
    is_second = half == 1
    left_old, right_old = left_stats[0], right_stats[0]
    left_root, right_root = left_roots[0], right_roots[0]

    def piece(step):
        return lax.dynamic_slice(gradient, (0, (column ^ step) * order), (rows, order))

    pieces = [piece(step) for step in range(chips)]
    mine = [pieces[0]] + [permute(pieces[step], chip_pairs(step)) for step in range(1, chips)]
    given_stat = jnp.where(is_second, left_old, right_old).astype(BF16)
    left_other, right_other, old_other = [permute(x, core_pairs()) for x in (left_root, right_root, given_stat)]
    other = [permute(x, core_pairs()) for x in mine]

    def shape(r, c, t):
        return jax.ShapeDtypeStruct((r, c), t)

    def kernel(f, *static):
        return lambda *refs: f(*static, *refs)

    left_rows, right_full, old_side = call(
        kernel(prepare, chips, rows, order),
        (shape(span, order, BF16), shape(order, order, BF16), shape(order, order, F32)),
        [pltpu.VMEM((order, order), BF16)],
        (0, 4 * order * order * 2),
    )(left_root, left_other, right_root, right_other, left_old, right_old, old_other.astype(F32))
    *updates, whole = call(
        kernel(precondition, chips, rows, order),
        (*[shape(rows, order, BF16)] * chips, shape(order, order, BF16)),
        [],
        (3 * order**3, 4 * order * order * 2),
    )(*mine, *other, left_rows, right_full)
    returned = [updates[0]] + [permute(updates[step], chip_pairs(step)) for step in range(1, chips)]
    left_new, right_new, root_mine, root_other = call(
        kernel(refreshed, order),
        (shape(span, order, F32), shape(span, order, F32), shape(span, order, BF16), shape(span, order, BF16)),
        [pltpu.VMEM((order, order), F32), pltpu.VMEM((order, order), F32), pltpu.VMEM((order, order), BF16)],
        (20 * order**3, 8 * order * order * 4),
    )(whole, left_old, right_old, old_side)
    taken = permute(root_other, core_pairs())
    listed = jnp.any(refresh[0] == column)
    left_out = jnp.where(listed, jnp.where(is_second, taken, root_mine), left_root)
    right_out = jnp.where(listed, jnp.where(is_second, root_mine, taken), right_root)
    update = jnp.zeros((rows, chips * order), BF16)
    for step in range(chips):
        update = lax.dynamic_update_slice(update, returned[step], (0, (column ^ step) * order))
    return (update, left_new[None], right_new[None], left_out[None], right_out[None])


def solution(mesh):
    block = P("brow", "bcol", None)
    rows = P(("brow", "bcol"), None)
    in_specs = (rows, block, block, block, block, P("brow", None))
    out_specs = (rows, block, block, block, block)
    return jax.shard_map(step, mesh=mesh, in_specs=in_specs, out_specs=out_specs, check_vma=False)
```

```python
import jax
import jax.numpy as jnp
from jax import lax
from jax.experimental import pallas as pl
from jax.experimental.pallas import tpu as pltpu
from jax.sharding import PartitionSpec as P

ITERS = 3
decay = 0.9
epsilon = 1e-06
F32 = jnp.float32
BF16 = jnp.bfloat16
ANY = pl.BlockSpec(memory_space=pl.ANY)
VMEM = pl.BlockSpec(memory_space=pltpu.VMEM)
SMEM = pl.BlockSpec(memory_space=pltpu.SMEM)


def place():
    position = lax.axis_index("bcol")
    return position >> 1, position & 1


def chip_pairs(step):
    return [(i, i ^ (step << 1)) for i in range(lax.axis_size("bcol"))]


def core_pairs():
    return [(i, i ^ 1) for i in range(lax.axis_size("bcol"))]


def permute(value, pairs):
    return lax.ppermute(value, "bcol", pairs)


def dot(left_side, right_side, contract=((1,), (0,))):
    return lax.dot_general(left_side, right_side, (contract, ((), ())), preferred_element_type=F32)


def call(kernel, out_shape, scratch, cost, ins=None, outs=None):
    flops, moved = cost

    def run(*operands):
        return pl.pallas_call(
            kernel,
            out_shape=out_shape,
            in_specs=ins or [VMEM] * len(operands),
            out_specs=outs or jax.tree.map(lambda _: VMEM, out_shape),
            scratch_shapes=scratch,
            compiler_params=pltpu.CompilerParams(vmem_limit_bytes=16 << 20),
            cost_estimate=pl.CostEstimate(flops=flops, bytes_accessed=moved, transcendentals=0),
        )(*operands)

    return run


def cut(chips, order, gradient, *refs):
    pieces, arrived = refs[:chips], refs[chips]
    column, _ = place()
    copies = []
    for step in sending(chips):
        start = pl.multiple_of((column ^ step) * order, order)
        copies.append(pltpu.make_async_copy(gradient.at[:, pl.ds(start, order)], pieces[step], arrived.at[step]))
    for copy in copies:
        copy.start()
    for copy in copies:
        copy.wait()


def sending(chips):
    return arrival(chips) + [0]


def deliver(chips, order, *refs):
    refresh, left_root, right_root, mine, taken = refs[:5]
    pieces, refs = refs[5 : 5 + chips], refs[5 + chips :]
    update, left_out, right_out, done = refs
    column, half = place()
    copies = []
    for step in range(chips):
        start = pl.multiple_of((column ^ step) * order, order)
        copies.append(pltpu.make_async_copy(pieces[step], update.at[:, pl.ds(start, order)], done.at[2 + step]))
    for copy in copies:
        copy.start()
    listed = refresh[0, 0] == column
    for entry in range(1, refresh.shape[1]):
        listed = jnp.logical_or(listed, refresh[0, entry] == column)
    first = jnp.logical_and(listed, half == 0)
    second = jnp.logical_and(listed, half == 1)

    def put(left, right):
        pltpu.make_async_copy(left, left_out, done.at[0]).start()
        pltpu.make_async_copy(right, right_out, done.at[1]).start()

    @pl.when(first)
    def _():
        put(mine, taken)

    @pl.when(second)
    def _():
        put(taken, mine)

    @pl.when(jnp.logical_not(listed))
    def _():
        put(left_root, right_root)

    pltpu.make_async_copy(mine, left_out, done.at[0]).wait()
    pltpu.make_async_copy(mine, right_out, done.at[1]).wait()
    for copy in copies:
        copy.wait()


def spans(chips):
    last = arrival(chips)[-2:]
    first = [(step, 0) for step in range(chips)] + [(step, 1) for step in range(chips) if step not in last]
    return first, [(step, 1) for step in last]


def row_of(piece, column, half, rows):
    step, other = piece
    return pl.ds(pl.multiple_of(((column ^ step) * 2 + (half ^ other)) * rows, rows), rows)


def prepare(chips, rows, order, left_mine, left_other, right_mine, right_other, old_left, old_right, old_other,
            left_first, left_last, right_full, left_kept, right_kept, other_kept, left_full, first_rows, last_rows,
            first_turned, last_turned):
    column, half = place()
    span = order // 2
    mine = pl.ds(pl.multiple_of(half * span, span), span)
    other = pl.ds(pl.multiple_of((1 - half) * span, span), span)
    left_full[mine, :] = left_mine[...]
    left_full[other, :] = left_other[...]
    right_full[mine, :] = right_mine[...]
    right_full[other, :] = right_other[...]
    groups = zip(spans(chips), (first_rows, last_rows), (first_turned, last_turned), (left_first, left_last))
    for pieces, gathered, turned, target in groups:
        for place_in, piece in enumerate(pieces):
            gathered[place_in * rows : (place_in + 1) * rows, :] = left_full[row_of(piece, column, half, rows), :]
        turned[...] = jnp.transpose(gathered[...])
        for step in range(chips):
            target[step * rows : (step + 1) * rows, :] = turned[row_of((step, 0), column, half, rows), :]
    left_kept[...] = decay * old_left[...]
    right_kept[...] = decay * old_right[...]
    other_kept[...] = decay * old_other[...].astype(F32)


def start_update(pieces, *refs):
    parts, (left_first, right_full, partial, block) = refs[: len(pieces)], refs[len(pieces) :]
    rows = parts[0].shape[0]
    for place_in, part in enumerate(parts):
        block[place_in * rows : (place_in + 1) * rows, :] = part[...]
    mixed = dot(block[...], right_full[...]).astype(BF16)
    partial[...] = dot(left_first[...], mixed)


def finish_update(pieces, chips, *refs):
    parts, refs = refs[: len(pieces)], refs[len(pieces) :]
    left_last, right_full, partial = refs[:3]
    updates, block = refs[3 : 3 + chips], refs[3 + chips]
    rows = parts[0].shape[0]
    for place_in, part in enumerate(parts):
        block[place_in * rows : (place_in + 1) * rows, :] = part[...]
    mixed = dot(block[...], right_full[...]).astype(BF16)
    result = (partial[...] + dot(left_last[...], mixed)).astype(BF16)
    for step in range(chips):
        updates[step][...] = result[step * rows : (step + 1) * rows, :]


def powers(moment):
    narrow = moment.astype(BF16)
    square = dot(narrow, narrow)
    return square, dot(square.astype(BF16), narrow), narrow


def refreshed(order, chips, *refs):
    parts, refs = refs[: 2 * chips], refs[2 * chips :]
    refreshed_body(order, parts, *refs)


def refreshed_body(order, parts, left_kept, right_kept, other_kept, left_out, right_out, root_mine, root_other,
                   whole, new_left, new_right, stat, root, done):
    column, half = place()
    chips, rows = len(parts) // 2, parts[0].shape[0]
    for which, part in enumerate(parts):
        whole[row_of((which % chips, which // chips), column, half, rows), :] = part[...]
    span = order // 2
    mine = pl.ds(pl.multiple_of(half * span, span), span)
    other = pl.ds(pl.multiple_of((1 - half) * span, span), span)
    rate = 1.0 - decay
    full = whole[...]
    new_left[...] = left_kept[...] + rate * dot(whole[mine, :], full, ((1,), (1,)))
    left_copy = pltpu.make_async_copy(new_left, left_out, done.at[0])
    left_copy.start()
    new_right[...] = right_kept[...] + rate * dot(whole[:, mine], full, ((0,), (0,)))
    right_copy = pltpu.make_async_copy(new_right, right_out, done.at[1])
    right_copy.start()

    @pl.when(half == 0)
    def _():
        stat[mine, :] = new_left[...]
        stat[other, :] = other_kept[...] + rate * dot(whole[other, :], full, ((1,), (1,)))

    @pl.when(half == 1)
    def _():
        stat[mine, :] = new_right[...]
        stat[other, :] = other_kept[...] + rate * dot(whole[:, other], full, ((0,), (0,)))

    shape = (order, order)
    diagonal = lax.broadcasted_iota(jnp.int32, shape, 0) == lax.broadcasted_iota(jnp.int32, shape, 1)
    shifted = stat[...] + jnp.where(diagonal, epsilon, 0.0)
    total = jnp.sum(jnp.sum(shifted * shifted, axis=1, keepdims=True), axis=0, keepdims=True)
    scaling = 2.5 / jnp.sqrt(total)
    moment = scaling * shifted
    first = moment
    for _ in range(ITERS - 2):
        square, cube, narrow = powers(moment)
        small = (20.0 / -256.0) * moment + (1.0 / 256.0) * square
        moment = (
            (625.0 / 256.0) * moment
            - (500.0 / 256.0) * square
            + (150.0 / 256.0) * cube
            + dot(cube.astype(BF16), small.astype(BF16))
        )
    square, cube, narrow = powers(moment)
    small = (250.0 / 4096.0) * moment - (25.0 / 4096.0) * square + (1.0 / 4096.0) * cube
    rest = (
        (-0.3125 - 3125.0 / 4096.0) * moment
        + (3125.0 / 4096.0) * square
        - (1250.0 / 4096.0) * cube
        + dot(cube.astype(BF16), small.astype(BF16))
    )
    product = dot(rest.astype(BF16), first.astype(BF16))
    result = 1.25 * rest - (0.25 * 1.5625) * first - 0.25 * product + jnp.where(diagonal, 1.25 * 1.5625, 0.0)
    root[...] = (jnp.sqrt(jnp.sqrt(scaling)) * result).astype(BF16)
    root_mine[...] = root[mine, :]
    root_other[...] = root[other, :]
    left_copy.wait()
    right_copy.wait()


def step(gradient, left_stats, right_stats, left_roots, right_roots, refresh):
    _, half = place()
    chips = lax.axis_size("bcol") // 2
    rows = gradient.shape[0]
    order = left_stats.shape[2]
    span = order // 2
    is_second = half == 1
    left_old, right_old = left_stats[0], right_stats[0]
    left_root, right_root = left_roots[0], right_roots[0]

    def shape(r, c, t):
        return jax.ShapeDtypeStruct((r, c), t)

    def kernel(f, *static):
        return lambda *refs: f(*static, *refs)

    def signals(count):
        return pltpu.SemaphoreType.DMA((count,))

    pieces = call(
        kernel(cut, chips, order), [shape(rows, order, BF16)] * chips, [signals(chips)], (0, rows * chips * order * 4),
        [ANY],
    )(gradient)
    mine = [pieces[0]] + [permute(pieces[step], chip_pairs(step)) for step in range(1, chips)]
    given_stat = jnp.where(is_second, left_old, right_old).astype(BF16)
    left_other, right_other, old_other = [permute(x, core_pairs()) for x in (left_root, right_root, given_stat)]
    other = [permute(x, core_pairs()) for x in mine]

    first, last = spans(chips)
    wide = [len(pieces) * rows for pieces in (first, last)]
    left_first, left_last, right_full, left_kept, right_kept, other_kept = call(
        kernel(prepare, chips, rows, order),
        (shape(span, wide[0], BF16), shape(span, wide[1], BF16), shape(order, order, BF16), *[shape(span, order, F32)] * 3),
        [pltpu.VMEM((order, order), BF16)]
        + [pltpu.VMEM((width, order), BF16) for width in wide]
        + [pltpu.VMEM((order, width), BF16) for width in wide],
        (0, 4 * order * order * 2),
    )(left_root, left_other, right_root, right_other, left_old, right_old, old_other)
    held = (mine, other)
    partial = call(
        kernel(start_update, first),
        shape(span, order, F32),
        [pltpu.VMEM((wide[0], order), BF16)],
        (3 * wide[0] * order**2, 4 * order * order * 2),
    )(*[held[side][step] for step, side in first], left_first, right_full)
    updates = call(
        kernel(finish_update, last, chips),
        [shape(rows, order, BF16)] * chips,
        [pltpu.VMEM((wide[1], order), BF16)],
        (3 * wide[1] * order**2, 4 * order * order * 2),
    )(*[held[side][step] for step, side in last], left_last, right_full, partial)
    returned = [updates[0]] + [permute(updates[step], chip_pairs(step)) for step in range(1, chips)]
    left_new, right_new, root_mine, root_other = call(
        kernel(refreshed, order, chips),
        (shape(span, order, F32), shape(span, order, F32), shape(span, order, BF16), shape(span, order, BF16)),
        [
            pltpu.VMEM((order, order), BF16),
            pltpu.VMEM((span, order), F32),
            pltpu.VMEM((span, order), F32),
            pltpu.VMEM((order, order), F32),
            pltpu.VMEM((order, order), BF16),
            signals(2),
        ],
        (20 * order**3, 8 * order * order * 4),
        None,
        (ANY, ANY, VMEM, VMEM),
    )(*mine, *other, left_kept, right_kept, other_kept)
    taken = permute(root_other, core_pairs())
    update, left_out, right_out = call(
        kernel(deliver, chips, order),
        (shape(rows, chips * order, BF16), shape(span, order, BF16), shape(span, order, BF16)),
        [signals(2 + chips)],
        (0, 4 * rows * chips * order * 4),
        [SMEM] + [VMEM] * (4 + chips),
        (ANY, ANY, ANY),
    )(refresh, left_root, right_root, root_mine, taken, *returned)
    return (update, left_new[None], right_new[None], left_out[None], right_out[None])


def arrival(chips):
    return list(range(chips // 2, chips)) + list(range(1, chips // 2))


def solution(mesh):
    block = P("brow", "bcol", None)
    rows = P(("brow", "bcol"), None)
    in_specs = (rows, block, block, block, block, P("brow", None))
    out_specs = (rows, block, block, block, block)
    return jax.shard_map(step, mesh=mesh, in_specs=in_specs, out_specs=out_specs, check_vma=False)
```

```python
import jax
import jax.numpy as jnp
from jax import lax
from jax.experimental import pallas as pl
from jax.experimental.pallas import tpu as pltpu
from jax.sharding import PartitionSpec as P

ITERS = 3
decay = 0.9
epsilon = 1e-06
F32 = jnp.float32
BF16 = jnp.bfloat16
ANY = pl.BlockSpec(memory_space=pl.ANY)
VMEM = pl.BlockSpec(memory_space=pltpu.VMEM)
SMEM = pl.BlockSpec(memory_space=pltpu.SMEM)


def place():
    position = lax.axis_index("bcol")
    return position >> 1, position & 1


def chip_pairs(step):
    return [(i, i ^ (step << 1)) for i in range(lax.axis_size("bcol"))]


def core_pairs():
    return [(i, i ^ 1) for i in range(lax.axis_size("bcol"))]


def permute(value, pairs):
    return lax.ppermute(value, "bcol", pairs)


def dot(left_side, right_side, contract=((1,), (0,))):
    return lax.dot_general(left_side, right_side, (contract, ((), ())), preferred_element_type=F32)


def call(kernel, out_shape, scratch, cost, ins=None, outs=None):
    flops, moved = cost

    def run(*operands):
        return pl.pallas_call(
            kernel,
            out_shape=out_shape,
            in_specs=ins or [VMEM] * len(operands),
            out_specs=outs or jax.tree.map(lambda _: VMEM, out_shape),
            scratch_shapes=scratch,
            compiler_params=pltpu.CompilerParams(vmem_limit_bytes=16 << 20),
            cost_estimate=pl.CostEstimate(flops=flops, bytes_accessed=moved, transcendentals=0),
        )(*operands)

    return run


def cut(chips, order, gradient, *refs):
    pieces, arrived = refs[:chips], refs[chips]
    column, _ = place()
    copies = []
    for step in sending(chips):
        start = pl.multiple_of((column ^ step) * order, order)
        copies.append(pltpu.make_async_copy(gradient.at[:, pl.ds(start, order)], pieces[step], arrived.at[step]))
    for copy in copies:
        copy.start()
    for copy in copies:
        copy.wait()


def sending(chips):
    return arrival(chips) + [0]


def deliver(chips, order, *refs):
    refresh, left_root, right_root, mine, taken = refs[:5]
    pieces, refs = refs[5 : 5 + chips], refs[5 + chips :]
    update, left_out, right_out, done = refs
    column, half = place()
    copies = []
    for step in range(chips):
        start = pl.multiple_of((column ^ step) * order, order)
        copies.append(pltpu.make_async_copy(pieces[step], update.at[:, pl.ds(start, order)], done.at[2 + step]))
    for copy in copies:
        copy.start()
    listed = refresh[0, 0] == column
    for entry in range(1, refresh.shape[1]):
        listed = jnp.logical_or(listed, refresh[0, entry] == column)
    first = jnp.logical_and(listed, half == 0)
    second = jnp.logical_and(listed, half == 1)

    def put(left, right):
        pltpu.make_async_copy(left, left_out, done.at[0]).start()
        pltpu.make_async_copy(right, right_out, done.at[1]).start()

    @pl.when(first)
    def _():
        put(mine, taken)

    @pl.when(second)
    def _():
        put(taken, mine)

    @pl.when(jnp.logical_not(listed))
    def _():
        put(left_root, right_root)

    pltpu.make_async_copy(mine, left_out, done.at[0]).wait()
    pltpu.make_async_copy(mine, right_out, done.at[1]).wait()
    for copy in copies:
        copy.wait()


def spans(chips):
    last = arrival(chips)[-2:]
    first = [(step, 0) for step in range(chips)] + [(step, 1) for step in range(chips) if step not in last]
    return first, [(step, 1) for step in last]


def row_of(piece, column, half, rows):
    step, other = piece
    return pl.ds(pl.multiple_of(((column ^ step) * 2 + (half ^ other)) * rows, rows), rows)


def prepare(chips, rows, order, left_mine, right_mine, old_left, old_right, packed,
            own_other, left_first, left_last, right_full, left_kept, right_kept, left_full, first_rows,
            last_rows, first_turned, last_turned):
    column, half = place()
    span = order // 2
    mine = pl.ds(pl.multiple_of(half * span, span), span)
    other = pl.ds(pl.multiple_of((1 - half) * span, span), span)
    left_full[mine, :] = left_mine[...]
    own_other[...] = packed[0:rows, :]
    left_full[other, :] = packed[rows : rows + span, :]
    right_full[mine, :] = right_mine[...]
    right_full[other, :] = packed[rows + span : rows + 2 * span, :]
    groups = zip(spans(chips), (first_rows, last_rows), (first_turned, last_turned), (left_first, left_last))
    for pieces, gathered, turned, target in groups:
        for place_in, piece in enumerate(pieces):
            gathered[place_in * rows : (place_in + 1) * rows, :] = left_full[row_of(piece, column, half, rows), :]
        turned[...] = jnp.transpose(gathered[...])
        for step in range(chips):
            target[step * rows : (step + 1) * rows, :] = turned[row_of((step, 0), column, half, rows), :]
    left_kept[...] = decay * old_left[...]
    right_kept[...] = decay * old_right[...]


def start_update(pieces, *refs):
    parts, (left_first, right_full, partial, block) = refs[: len(pieces)], refs[len(pieces) :]
    rows = parts[0].shape[0]
    for place_in, part in enumerate(parts):
        block[place_in * rows : (place_in + 1) * rows, :] = part[...]
    mixed = dot(block[...], right_full[...]).astype(BF16)
    partial[...] = dot(left_first[...], mixed)


def finish_update(pieces, chips, *refs):
    parts, refs = refs[: len(pieces)], refs[len(pieces) :]
    left_last, right_full, partial = refs[:3]
    updates, block = refs[3 : 3 + chips], refs[3 + chips]
    rows = parts[0].shape[0]
    for place_in, part in enumerate(parts):
        block[place_in * rows : (place_in + 1) * rows, :] = part[...]
    mixed = dot(block[...], right_full[...]).astype(BF16)
    result = (partial[...] + dot(left_last[...], mixed)).astype(BF16)
    for step in range(chips):
        updates[step][...] = result[step * rows : (step + 1) * rows, :]


def powers(moment):
    narrow = moment.astype(BF16)
    square = dot(narrow, narrow)
    return square, dot(square.astype(BF16), narrow), narrow


def refreshed(order, chips, *refs):
    parts, refs = refs[: 2 * chips], refs[2 * chips :]
    refreshed_body(order, parts, *refs)


def refreshed_body(order, parts, left_kept, right_kept, old_other, left_out, right_out, root_mine, root_other,
                   whole, new_left, new_right, stat, root, done):
    column, half = place()
    chips, rows = len(parts) // 2, parts[0].shape[0]
    for which, part in enumerate(parts):
        whole[row_of((which % chips, which // chips), column, half, rows), :] = part[...]
    span = order // 2
    mine = pl.ds(pl.multiple_of(half * span, span), span)
    other = pl.ds(pl.multiple_of((1 - half) * span, span), span)
    rate = 1.0 - decay
    full = whole[...]
    new_left[...] = left_kept[...] + rate * dot(whole[mine, :], full, ((1,), (1,)))
    left_copy = pltpu.make_async_copy(new_left, left_out, done.at[0])
    left_copy.start()
    new_right[...] = right_kept[...] + rate * dot(whole[:, mine], full, ((0,), (0,)))
    right_copy = pltpu.make_async_copy(new_right, right_out, done.at[1])
    right_copy.start()

    @pl.when(half == 0)
    def _():
        stat[mine, :] = new_left[...]
        stat[other, :] = decay * old_other[...].astype(F32) + rate * dot(whole[other, :], full, ((1,), (1,)))

    @pl.when(half == 1)
    def _():
        stat[mine, :] = new_right[...]
        stat[other, :] = decay * old_other[...].astype(F32) + rate * dot(whole[:, other], full, ((0,), (0,)))

    shape = (order, order)
    diagonal = lax.broadcasted_iota(jnp.int32, shape, 0) == lax.broadcasted_iota(jnp.int32, shape, 1)
    shifted = stat[...] + jnp.where(diagonal, epsilon, 0.0)
    total = jnp.sum(jnp.sum(shifted * shifted, axis=1, keepdims=True), axis=0, keepdims=True)
    scaling = 2.5 / jnp.sqrt(total)
    moment = scaling * shifted
    first = moment
    for _ in range(ITERS - 2):
        square, cube, narrow = powers(moment)
        small = (20.0 / -256.0) * moment + (1.0 / 256.0) * square
        moment = (
            (625.0 / 256.0) * moment
            - (500.0 / 256.0) * square
            + (150.0 / 256.0) * cube
            + dot(cube.astype(BF16), small.astype(BF16))
        )
    square, cube, narrow = powers(moment)
    small = (250.0 / 4096.0) * moment - (25.0 / 4096.0) * square + (1.0 / 4096.0) * cube
    rest = (
        (-0.3125 - 3125.0 / 4096.0) * moment
        + (3125.0 / 4096.0) * square
        - (1250.0 / 4096.0) * cube
        + dot(cube.astype(BF16), small.astype(BF16))
    )
    product = dot(rest.astype(BF16), first.astype(BF16))
    result = 1.25 * rest - (0.25 * 1.5625) * first - 0.25 * product + jnp.where(diagonal, 1.25 * 1.5625, 0.0)
    root[...] = (jnp.sqrt(jnp.sqrt(scaling)) * result).astype(BF16)
    root_mine[...] = root[mine, :]
    root_other[...] = root[other, :]
    left_copy.wait()
    right_copy.wait()


def step(gradient, left_stats, right_stats, left_roots, right_roots, refresh):
    _, half = place()
    chips = lax.axis_size("bcol") // 2
    rows = gradient.shape[0]
    order = left_stats.shape[2]
    span = order // 2
    left_old, right_old = left_stats[0], right_stats[0]
    left_root, right_root = left_roots[0], right_roots[0]

    def shape(r, c, t):
        return jax.ShapeDtypeStruct((r, c), t)

    def kernel(f, *static):
        return lambda *refs: f(*static, *refs)

    def signals(count):
        return pltpu.SemaphoreType.DMA((count,))

    pieces = call(
        kernel(cut, chips, order), [shape(rows, order, BF16)] * chips, [signals(chips)], (0, rows * chips * order * 4),
        [ANY],
    )(gradient)
    mine = [pieces[0]] + [permute(pieces[step], chip_pairs(step)) for step in range(1, chips)]
    given_stat = jnp.where(half == 1, left_old, right_old).astype(BF16)
    packed = jnp.concatenate([pieces[0], left_root, right_root], 0)
    packed = permute(packed, core_pairs())
    old_other = permute(given_stat, core_pairs())
    first, last = spans(chips)
    wide = [len(pieces) * rows for pieces in (first, last)]
    own_other, left_first, left_last, right_full, left_kept, right_kept = call(
        kernel(prepare, chips, rows, order),
        (shape(rows, order, BF16), shape(span, wide[0], BF16), shape(span, wide[1], BF16), shape(order, order, BF16), *[shape(span, order, F32)] * 2),
        [pltpu.VMEM((order, order), BF16)]
        + [pltpu.VMEM((width, order), BF16) for width in wide]
        + [pltpu.VMEM((order, width), BF16) for width in wide],
        (0, 4 * order * order * 2),
    )(left_root, right_root, left_old, right_old, packed)
    other = [own_other] + [permute(mine[step], core_pairs()) for step in range(1, chips)]
    held = (mine, other)
    partial = call(
        kernel(start_update, first),
        shape(span, order, F32),
        [pltpu.VMEM((wide[0], order), BF16)],
        (3 * wide[0] * order**2, 4 * order * order * 2),
    )(*[held[side][step] for step, side in first], left_first, right_full)
    updates = call(
        kernel(finish_update, last, chips),
        [shape(rows, order, BF16)] * chips,
        [pltpu.VMEM((wide[1], order), BF16)],
        (3 * wide[1] * order**2, 4 * order * order * 2),
    )(*[held[side][step] for step, side in last], left_last, right_full, partial)
    returned = [updates[0]] + [permute(updates[step], chip_pairs(step)) for step in range(1, chips)]
    left_new, right_new, root_mine, root_other = call(
        kernel(refreshed, order, chips),
        (shape(span, order, F32), shape(span, order, F32), shape(span, order, BF16), shape(span, order, BF16)),
        [
            pltpu.VMEM((order, order), BF16),
            pltpu.VMEM((span, order), F32),
            pltpu.VMEM((span, order), F32),
            pltpu.VMEM((order, order), F32),
            pltpu.VMEM((order, order), BF16),
            signals(2),
        ],
        (20 * order**3, 8 * order * order * 4),
        None,
        (ANY, ANY, VMEM, VMEM),
    )(*mine, *other, left_kept, right_kept, old_other)
    taken = permute(root_other, core_pairs())
    update, left_out, right_out = call(
        kernel(deliver, chips, order),
        (shape(rows, chips * order, BF16), shape(span, order, BF16), shape(span, order, BF16)),
        [signals(2 + chips)],
        (0, 4 * rows * chips * order * 4),
        [SMEM] + [VMEM] * (4 + chips),
        (ANY, ANY, ANY),
    )(refresh, left_root, right_root, root_mine, taken, *returned)
    return (update, left_new[None], right_new[None], left_out[None], right_out[None])


def arrival(chips):
    return list(range(chips - 1, 0, -1))


def solution(mesh):
    block = P("brow", "bcol", None)
    rows = P(("brow", "bcol"), None)
    in_specs = (rows, block, block, block, block, P("brow", None))
    out_specs = (rows, block, block, block, block)
    return jax.shard_map(step, mesh=mesh, in_specs=in_specs, out_specs=out_specs, check_vma=False)
```
